256 devices in a mesh: tm: 64 (over y, z_hi, x), neur: 4 (over z_lo, core).
Axes of the slice: x: 4, y: 4, z: 8 (z_hi: 4, z_lo: 2; z = z_hi * 2 + z_lo), core: 2. Of those that a mesh axis runs over, the one named last changes fastest.
Arguments:
- recording: bfloat16 [2048, 16384], P('neur', 'tm'), may hold values from -6 to 6
- motifs: bfloat16 [128, 64, 2048], P(None, None, 'neur'), may hold values from -0.0625 to 0.0625
- loadings: bfloat16 [64, 16384], P(None, 'tm'), may hold values from -6 to 6
Outputs:
- grad_motifs: float32 [128, 64, 2048], P('tm', None, 'neur')
- grad_loadings: float32 [64, 16384], P(None, 'tm')
The draws below stay inside these ranges and needn't reach their ends.
All inputs are finite; a program needn't handle non-finite values.
Results may differ from the reference program's by a relative error of at most 0.0021.
Values may be sent and summed in bfloat16 or wider, within the bound.
A program may use at most 128 MiB of HBM per device.

```python
import math
import jax
import jax.numpy as jnp
from jax import lax

MOTIFS = 64
LAGS = 128
NEURONS = 2048
TIME = 16384


def shard_levels(rng, extent, shards, low, top_value):
    def one(position, parts):
        heights = jax.random.uniform(jax.random.fold_in(jax.random.fold_in(rng, 6), position), (parts,), jnp.float32, low / len(shards), top_value / len(shards))
        return jnp.repeat(jnp.exp(heights), extent[position] // parts).reshape((-1,) + (1,) * (len(extent) - position - 1))

    loudness = one(*shards[0])
    for cut in shards[1:]:
        loudness = loudness * one(*cut)
    return loudness


def bell_draw(rng, shape, scale, most, pieces=(), kind=jnp.bfloat16):
    array = scale * jax.random.normal(rng, shape, jnp.float32)
    if pieces:
        array = array * shard_levels(rng, shape, pieces, -0.22, 0.18)
    return jnp.clip(array, -most, most).astype(kind)


def setup_inputs(seed: int = 0) -> dict:
    keys = jax.random.split(jax.random.key(seed), 4)
    recording = bell_draw(keys[0], (NEURONS, TIME), 1.0, 6.0, ((0, 4), (1, 64)))
    motifs = bell_draw(keys[1], (LAGS, MOTIFS, NEURONS), (LAGS * MOTIFS) ** -0.5, 0.0625, ((2, 4),))
    loadings = bell_draw(keys[2], (MOTIFS, TIME), 1.0, 6.0, ((1, 64),))
    return {"recording": recording, "motifs": motifs, "loadings": loadings}


def reference(recording, motifs, loadings):
    padded_load = jnp.concatenate([jnp.zeros((MOTIFS, LAGS), jnp.bfloat16), loadings], axis=1)

    def lagged(lag_value):
        return lax.dynamic_slice_in_dim(padded_load, LAGS - lag_value, TIME, 1)

    def add_forward(lag_value, running):
        weight_lag = lax.dynamic_index_in_dim(motifs, lag_value, 0, keepdims=False)
        return running + jnp.dot(weight_lag.T, lagged(lag_value), preferred_element_type=jnp.float32)
    rebuilt = lax.fori_loop(0, LAGS, add_forward, jnp.zeros((NEURONS, TIME), jnp.float32))
    residual = (rebuilt - recording.astype(jnp.float32)).astype(jnp.bfloat16)
    residual_t = residual.T

    def motif_grad(lag_value):
        return jnp.dot(lagged(lag_value), residual_t, preferred_element_type=jnp.float32)
    grad_motifs = lax.map(motif_grad, jnp.arange(LAGS, dtype=jnp.int32)) * (1.0 / math.sqrt(TIME))
    padded_res = jnp.concatenate([residual, jnp.zeros((NEURONS, LAGS), jnp.bfloat16)], axis=1)

    def add_backward(lag_value, running):
        weight_lag = lax.dynamic_index_in_dim(motifs, lag_value, 0, keepdims=False)
        ahead_cols = lax.dynamic_slice_in_dim(padded_res, lag_value, TIME, 1)
        return running + jnp.dot(weight_lag, ahead_cols, preferred_element_type=jnp.float32)
    grad_sum = lax.fori_loop(0, LAGS, add_backward, jnp.zeros((MOTIFS, TIME), jnp.float32))
    grad_loadings = grad_sum * math.sqrt(MOTIFS / NEURONS)
    return (grad_motifs, grad_loadings)
```

```python
import functools
import math

import jax
import jax.numpy as jnp
from jax import lax
from jax.experimental import pallas as pl
from jax.experimental.pallas import tpu as pltpu
from jax.sharding import PartitionSpec as P

F32 = jnp.float32
BF16 = jnp.bfloat16
NX = NY = NZ = 4
LAGS, K, N, T = 128, 64, 512, 256
J = 16
M = LAGS // J
Q = 256
OFFS = [32 * dy + 8 * pz + b for dy in range(2) for pz in range(NZ) for b in range(2)]


def kernel(
    glscale, gmscale, rec_hbm, w_hbm, load_hbm, gm_ref, gl_ref,
    rec_v, w_v, hext, hal, htp, x16, reb, rt, hb, rb, a_v, acc, p_v,
    gp, gr, gs, gh, glb, sz, zb, zf,
    load_sem, rec_sem, w_sem, hal_sem, send_sem, recv_sem, g_sem, g2_sem, z_send, z_recv, self_sem,
):
    tm = lax.axis_index("tm")
    ne = lax.axis_index("neur")
    tms = NX * NY * NZ
    x, zh, y = lax.rem(tm, NX), lax.rem(lax.div(tm, NX), NZ), lax.div(tm, NX * NZ)
    zl, c = lax.div(ne, 2), lax.rem(ne, 2)

    def dev(xx, yy, zz, ll, cc):
        return {"tm": (yy * NZ + zz) * NX + xx, "neur": ll * 2 + cc}

    def rc(src, dst, ssem, rsem, target):
        return pltpu.make_async_remote_copy(
            src_ref=src, dst_ref=dst, send_sem=ssem, recv_sem=rsem,
            device_id=target, device_id_type=pl.DeviceIdType.MESH,
        )

    def add(value, step, size):
        return lax.rem(value + step, size)

    own_cp = pltpu.make_async_copy(load_hbm, hext.at[:, pl.ds(128, T)], load_sem)
    own_cp.start()
    rec_cp = pltpu.make_async_copy(rec_hbm, rec_v, rec_sem)
    rec_cp.start()
    for m in range(M):
        pltpu.make_async_copy(w_hbm.at[m], w_v.at[m], w_sem.at[m]).start()

    barrier = pltpu.get_barrier_semaphore()
    greet = []
    for dy in range(NY):
        for dz in range(NZ):
            for dc in range(2):
                if dy or dz or dc:
                    greet.append(dev(x, add(y, dy, NY), add(zh, dz, NZ), zl, add(c, dc, 2)))
    for dx in (1, NX - 1):
        greet.append(dev(add(x, dx, NX), y, zh, zl, c))
    for dt in (1, tms - 1):
        greet.append({"tm": add(tm, dt, tms), "neur": ne})
    for dc in range(2):
        greet.append(dev(x, y, zh, 1 - zl, add(c, dc, 2)))
    for target in greet:
        pl.semaphore_signal(barrier, inc=1, device_id=target, device_id_type=pl.DeviceIdType.MESH)

    sends = []

    own_cp.wait()

    def build_htp(first):
        block = hext[:, first : first + 256].astype(F32)
        pair = jnp.concatenate([block, pltpu.roll(block, 1, 1)], axis=0)
        htp[first : first + 256] = pair.T

    def build_x16(first, rows):
        for p in range(J // 2):
            x16[pl.ds(first, rows), 128 * p : 128 * (p + 1)] = htp[
                first - 2 * p : first - 2 * p + rows
            ].astype(BF16)

    build_htp(128)
    build_x16(144, 240)
    reb[...] = jnp.zeros_like(reb)

    def forward(half, waits):
        def body(m, carry):
            if waits:
                pltpu.make_async_copy(w_hbm.at[m], w_v.at[m], w_sem.at[m]).wait()
            first = pl.multiple_of(128 + 128 * half - J * m, J)
            reb[pl.ds(128 * half, 128)] += jnp.dot(
                x16[pl.ds(first, 128)], w_v[m], preferred_element_type=F32
            )
            return carry

        lax.fori_loop(0, M, body, 0)
        rows = slice(128 * half, 128 * half + 128)
        rt[rows] = (reb[rows] - rec_v[:, rows].astype(F32).T).astype(BF16)

    forward_hi = functools.partial(forward, 1, True)

    pl.semaphore_wait(barrier, len(greet))
    halo = rc(
        hext.at[:, pl.ds(256, 128)], hal, hal_sem.at[0], hal_sem.at[1],
        {"tm": add(tm, 1, tms), "neur": ne},
    )
    halo.start()
    sends.append(halo)
    rec_cp.wait()
    forward_hi()

    def slot(q, kk, xs, i):
        if q == 0:
            return hb.at[(kk * NX + xs) * 2 + i]
        return rb.at[kk * NX + xs, pl.ds(pl.multiple_of(i * 256 + (q - 1) * 128, 128), 128)]

    def landed(q, kk, xs, i):
        return recv_sem.at[q, (kk * NX + xs) * 2 + i]

    def await_slot(q, kk, xs, i):
        ref = slot(q, kk, xs, i)
        rc(ref, ref, send_sem.at[q, 0], landed(q, kk, xs, i), dev(x, y, zh, zl, 1 - c)).wait_recv()

    def pass_on(q, kk, xs, i, number, target):
        ref = slot(q, kk, xs, i)
        copy = rc(ref, ref, send_sem.at[q, number], landed(q, kk, xs, i), target)
        copy.start()
        sends.append(copy)

    right = dev(add(x, 1, NX), y, zh, zl, c)
    left = dev(add(x, NX - 1, NX), y, zh, zl, c)
    sibling = dev(x, y, zh, zl, 1 - c)
    par, half_y = lax.rem(y, 2), lax.div(y, 2)
    y_waits = []

    def to_row(q):
        for h in range(2):
            if q == 0:
                src = hext
            else:
                src = rt.at[pl.ds(128 * (q - 1), 128), pl.ds(Q * h, Q)]
            dst = slot(q, par, x, half_y)
            sem = landed(q, par, x, half_y)
            remote = rc(src, dst, send_sem.at[q, h], sem, dev(x, 2 * c + h, zh, zl, par))
            local = pltpu.make_async_copy(src, dst, sem)
            is_self = jnp.logical_and(y == 2 * c + h, c == par)

            @pl.when(is_self)
            def _():
                local.start()

            @pl.when(jnp.logical_not(is_self))
            def _():
                remote.start()

            y_waits.append((is_self, remote))

    def hop0(q):
        for i in range(2):
            await_slot(q, c, x, i)
            pass_on(q, c, x, i, 2 + i, right)
            pass_on(q, c, x, i, 4 + i, left)
            pass_on(q, c, x, i, 6 + i, sibling)

    def hop1(q):
        xl, xr = add(x, NX - 1, NX), add(x, 1, NX)
        await_slot(q, c, xl, 0)
        pass_on(q, c, xl, 0, 8, right)
        pass_on(q, c, xl, 0, 9, sibling)
        await_slot(q, c, xr, 1)
        pass_on(q, c, xr, 1, 10, left)
        pass_on(q, c, xr, 1, 11, sibling)
        await_slot(q, c, xl, 1)
        pass_on(q, c, xl, 1, 12, sibling)
        await_slot(q, c, xr, 0)
        pass_on(q, c, xr, 0, 13, sibling)

    def hop2(q):
        xo = add(x, 2, NX)
        for i in range(2):
            await_slot(q, c, xo, i)
            pass_on(q, c, xo, i, 14 + i, sibling)

    def hop3(q, dx):
        for i in range(2):
            await_slot(q, 1 - c, add(x, dx, NX), i)

    to_row(2)
    halo.wait_recv()
    hext[:, 0:128] = jnp.where(tm == 0, jnp.zeros_like(hal[...], F32), hal[...].astype(F32)).astype(BF16)
    build_htp(0)
    build_x16(16, 128)
    to_row(0)
    forward(0, False)
    to_row(1)
    hop0(0)
    hop0(2)

    p_v[...] = jnp.zeros_like(p_v)

    def back(first, last):
        def body(m, carry):
            rows = pl.ds(pl.multiple_of(128 - J * m, J), T)
            p_v[rows] += lax.dot_general(
                rt[...], w_v[m], (((1,), (1,)), ((), ())), preferred_element_type=F32
            )
            return carry

        lax.fori_loop(first, last, body, 0)

    back(0, M // 2)
    hop0(1)
    hop1(0)
    hop1(2)
    back(M // 2, M)
    hop1(1)
    hop2(0)
    hop2(2)

    even = jnp.zeros((384, 128), F32)
    odd = jnp.zeros((384, 128), F32)
    for p in range(J // 2):
        lanes = slice(128 * p, 128 * (p + 1))
        even += p_v[2 * p : 2 * p + 384, lanes]
        odd += p_v[2 * p + 1 : 2 * p + 385, lanes]
    gp[...] = (even + pltpu.roll(odd, 64, 1)).T[0:K]

    def neur_at(d):
        return {"tm": tm, "neur": add(ne, d, 4)}

    for d in range(1, 4):
        rows = pl.ds(pl.multiple_of(add(ne, d, 4) * 16, 16), 16)
        copy = rc(gp.at[rows], gr.at[d - 1], g_sem.at[0, d - 1], g_sem.at[1, d - 1], neur_at(d))
        copy.start()
        sends.append(copy)
    hop2(1)

    for dx in range(NX):
        hop3(0, dx)
    base = 64 * c + 2 * x

    def build_a(idx, carry):
        rolled = pltpu.roll(hb[idx].astype(F32), base, 1)
        kx, i = lax.div(idx, 2), lax.rem(idx, 2)
        cols = pl.ds(pl.multiple_of(i * T, T), T)
        for o, off in enumerate(OFFS):
            moved = pltpu.roll(rolled, off, 1) if off else rolled
            a_v[kx, K * o : K * (o + 1), cols] = moved[:, 128:384].astype(BF16)
        return carry

    lax.fori_loop(0, 2 * 2 * NX, build_a, 0)

    mine = pl.ds(pl.multiple_of(ne * 16, 16), 16)
    total = gp[mine]
    for d in range(1, 4):
        rc(gr.at[d - 1], gr.at[d - 1], g_sem.at[0, d - 1], g_sem.at[1, d - 1], neur_at(d)).wait_recv()
        total += gr[d - 1]
    gs[...] = total
    edge = rc(
        gs.at[:, pl.ds(0, 128)], gh, g_sem.at[0, 3], g_sem.at[1, 3],
        {"tm": add(tm, tms - 1, tms), "neur": ne},
    )
    edge.start()
    sends.append(edge)

    order = [(c, add(x, dx, NX)) for dx in (0, 1, 3, 2)] + [(1 - c, add(x, dx, NX)) for dx in (0, 1, 3, 2)]
    dxs = (0, 1, 3, 2)
    for step, (kk, xs) in enumerate(order):
        if step >= 4:
            hop3(2, dxs[step - 4])
            hop3(1, dxs[step - 4])
        kx = kk * NX + xs
        part = jnp.dot(a_v[kx], rb[kx], preferred_element_type=F32)
        if step == 0:
            acc[...] = part
        else:
            acc[...] += part
        if step == 3:
            edge.wait_recv()
            last = gh[...]
            own = gs[:, 128:384]
            rest = jnp.where(tm == tms - 1, jnp.zeros_like(last), last)
            glb[mine] = (own + jnp.concatenate([jnp.zeros_like(last), rest], axis=1)) * glscale
            for d in range(1, 4):
                copy = rc(glb.at[mine], glb.at[mine], g2_sem.at[0, d - 1], g2_sem.at[1, d - 1], neur_at(d))
                copy.start()
                sends.append(copy)

    z_waits = []
    for dz in (2, 1, 3, 0):
        pz = add(zh, dz, NZ)
        for dy in range(2):
            rows = pl.ds(pl.multiple_of((dy * NZ + pz) * 128, 128), 128)
            target = dev(x, 2 * c + dy, pz, zl, half_y)
            if dz:
                sz[dy, dz - 1] = acc[rows].astype(BF16)
                copy = rc(
                    sz.at[dy, dz - 1], zb.at[par, dz - 1], z_send.at[dy, dz], z_recv.at[par, dz], target
                )
                copy.start()
                sends.append(copy)
            else:
                remote = rc(acc.at[rows], zf.at[par], z_send.at[dy, 0], z_recv.at[par, 0], target)
                local = pltpu.make_async_copy(acc.at[rows], zf.at[par], z_recv.at[par, 0])
                is_self = jnp.logical_and(half_y == c, par == dy)

                @pl.when(is_self)
                def _():
                    local.start()

                @pl.when(jnp.logical_not(is_self))
                def _():
                    remote.start()

                z_waits.append((is_self, remote))

    for d in range(1, 4):
        rows = pl.ds(pl.multiple_of(add(ne, 4 - d, 4) * 16, 16), 16)
        rc(glb.at[rows], glb.at[rows], g2_sem.at[0, d - 1], g2_sem.at[1, d - 1], neur_at(d)).wait_recv()
    gl_ref[...] = glb[...]

    for h in range(2):
        rc(zf.at[h], zf.at[h], z_send.at[0, 0], z_recv.at[h, 0], sibling).wait_recv()
        value = zf[h]
        for dz in (1, 3, 2):
            rc(zb.at[h, dz - 1], zb.at[h, dz - 1], z_send.at[0, dz], z_recv.at[h, dz], sibling).wait_recv()
            value += zb[h, dz - 1].astype(F32)
        value = value * gmscale
        for b in range(2):
            gm_ref[b, :, Q * h : Q * (h + 1)] = value[K * b : K * (b + 1)]

    for copy in sends:
        copy.wait_send()
    for is_self, copy in y_waits + z_waits:

        @pl.when(jnp.logical_not(is_self))
        def _():
            copy.wait_send()


def on_device(recording, motifs, loadings):
    neurons = recording.shape[0] * lax.axis_size("neur")
    total_time = recording.shape[1] * lax.axis_size("tm")
    glscale = math.sqrt(motifs.shape[1] / neurons)
    gmscale = 1.0 / math.sqrt(total_time)
    vm = pltpu.VMEM
    dma = pltpu.SemaphoreType.DMA
    return pl.pallas_call(
        functools.partial(kernel, glscale, gmscale),
        out_shape=(
            jax.ShapeDtypeStruct((2, K, N), F32),
            jax.ShapeDtypeStruct((K, T), F32),
        ),
        in_specs=[pl.BlockSpec(memory_space=pl.ANY)] * 3,
        out_specs=(pl.BlockSpec(memory_space=pltpu.VMEM),) * 2,
        scratch_shapes=[
            vm((N, T), BF16),
            vm((M, J * K, N), BF16),
            vm((K, 384), BF16),
            vm((K, 128), BF16),
            vm((384, 128), F32),
            vm((384, J * K), BF16),
            vm((T, N), F32),
            vm((T, N), BF16),
            vm((16, K, 384), BF16),
            vm((8, 2 * T, Q), BF16),
            vm((8, J * K, 2 * T), BF16),
            vm((J * K, Q), F32),
            vm((400, J * K), F32),
            vm((K, 384), F32),
            vm((3, 16, 384), F32),
            vm((16, 384), F32),
            vm((16, 128), F32),
            vm((K, T), F32),
            vm((2, 3, 128, Q), BF16),
            vm((2, 3, 128, Q), BF16),
            vm((2, 128, Q), F32),
            dma, dma, dma((M,)), dma((2,)), dma((3, 16)), dma((3, 16)), dma((2, 4)), dma((2, 3)),
            dma((2, 4)), dma((2, 4)), dma,
        ],
        compiler_params=pltpu.CompilerParams(
            collective_id=0, has_side_effects=True, vmem_limit_bytes=60 * 1024 * 1024
        ),
    )(recording, motifs.reshape(M, J * K, N), loadings)


def solution(mesh):
    in_specs = (P("neur", "tm"), P(None, None, "neur"), P(None, "tm"))
    out_specs = (P("tm", None, "neur"), P(None, "tm"))
    return jax.shard_map(
        on_device, mesh=mesh, in_specs=in_specs, out_specs=out_specs, check_vma=False
    )
```
